512 devices in a mesh: left: 4 (over y_lo, core), right: 16 (over x, y_hi), occ: 8 (over z).
Axes of the slice: x: 4, y: 8 (y_hi: 4, y_lo: 2; y = y_hi * 2 + y_lo), z: 8, core: 2. Of those that a mesh axis runs over, the one named last changes fastest.
Arguments:
- chol: bfloat16 [16, 1024, 2048], P('right', 'occ', 'left'), may hold values from -0.125 to 0.125
- amps: bfloat16 [4, 4, 1024, 512], P('left', None, 'occ', 'right'), may hold values from -1.5 to 1.5
- listed: int32 [4, 4, 4, 4], replicated, may hold values 0 or 1
Outputs:
- residual: float32 [4, 4, 1024, 512], P('left', None, 'occ', 'right')
The draws below stay inside these ranges and needn't reach their ends.
All inputs are finite; a program needn't handle non-finite values.
Results may differ from the reference program's by a relative error of at most 0.0029.
Values may be sent and summed in bfloat16 or wider, within the bound.
A program may use at most 64 MiB of HBM per device.

```python
import jax
import jax.numpy as jnp
from jax import lax

TV = 32
NTV = 4
NQ = 2048
NOP = 512
PAIR = 1024
NPT = 16


def place_ends(values, stream_key, smallest, top_value):
    longest = values.shape.index(max(values.shape))
    spots = []
    for shift in (0, 1):
        where = [jax.random.randint(jax.random.fold_in(stream_key, axis), (), 0, length) for axis, length in enumerate(values.shape)]
        where[longest] = (where[longest] + shift) % values.shape[longest]
        spots.append(tuple(where))
    return values.at[spots[0]].set(smallest).at[spots[1]].set(top_value)


def block_levels(rng, shape, shards, smallest, top_value):
    gain = 1.0
    for dim, shards_of in shards:
        heights = jax.random.uniform(jax.random.fold_in(jax.random.fold_in(rng, 6), dim), (shards_of,), jnp.float32, smallest / len(shards), top_value / len(shards))
        gain = gain * jnp.repeat(jnp.exp(heights), shape[dim] // shards_of).reshape((-1,) + (1,) * (len(shape) - 1 - dim))
    return gain


def noise(key, extent, deviation, most, pieces=(), kind=jnp.bfloat16):
    gain = block_levels(key, extent, pieces, -0.22, 0.18) if pieces else 1.0
    values = jax.random.normal(key, extent, jnp.float32) * deviation * gain
    return jnp.minimum(jnp.maximum(values, -most), most).astype(kind)


def setup_inputs(seed: int = 0) -> dict:
    key_list = jax.random.split(jax.random.key(seed), 4)
    chol = noise(key_list[0], (NPT, PAIR, NQ), NQ ** -0.5, 0.125, ((0, 16), (1, 8), (2, 4)))
    amps = noise(key_list[1], (NTV, NTV, PAIR, NOP), 0.25, 1.5, ((0, 4), (2, 8), (3, 16)))
    listed = place_ends((jax.random.randint(key_list[2], (NTV, NTV, NTV, NTV), 0, 4) < 3).astype(jnp.int32), jax.random.fold_in(key_list[2], 1), 0, 1)
    return {"chol": chol, "amps": amps, "listed": listed}


def reference(chol, amps, listed):
    tiles = chol.astype(jnp.float32).reshape(NTV, NTV, PAIR, NQ)
    amp_full = amps.astype(jnp.float32)
    live_all = listed.astype(jnp.float32)

    def one_block(block_index):
        a_tile = block_index // NTV
        b_tile = block_index % NTV

        def add_task(running, task_index):
            c_tile = task_index // NTV
            d_tile = task_index % NTV
            left_tile = tiles[a_tile, c_tile]
            right_tile = tiles[b_tile, d_tile]
            inner = jnp.dot(left_tile, right_tile.T, precision=lax.Precision.HIGHEST)
            inner = lax.optimization_barrier(inner.astype(jnp.bfloat16)).astype(jnp.float32)
            swapped = inner.reshape(TV, TV, TV, TV).transpose(0, 2, 1, 3).reshape(PAIR, PAIR)
            term = jnp.dot(swapped, amp_full[c_tile, d_tile], precision=lax.Precision.HIGHEST)
            return running + live_all[a_tile, c_tile, b_tile, d_tile] * term, None

        running, _ = lax.scan(add_task, jnp.zeros((PAIR, NOP), jnp.float32), jnp.arange(NTV * NTV).astype(jnp.int32))
        return running

    blocks = lax.map(one_block, jnp.arange(NTV * NTV).astype(jnp.int32))
    return blocks.reshape(NTV, NTV, PAIR, NOP)
```

```python
import jax
import jax.numpy as jnp
from jax import lax
from jax.experimental import pallas as pl
from jax.experimental.pallas import tpu as pltpu
from jax.sharding import PartitionSpec as P

NTV = 4
MESH = pl.DeviceIdType.MESH
NT = (((1,), (1,)), ((), ()))


def kernel(
    listed, chol, amps, out,
    bd, xb, pb, tb, v, w, rs, rr, rx, ob,
    bd_r, bdp_r, xb_r, pb_r, t1_r, t2_r, tx_r, tp_r, rr_r, ob_r,
    loc_s, y_s, z_s, x_s, bdp_s, pb_s, t1_s, t2_s, tx_s, tp_s, rr_s, ob_s,
):
    left = lax.axis_index("left")
    right = lax.axis_index("right")
    z = lax.axis_index("occ")
    yl, c = left // 2, left % 2
    x, yh = right // 4, right % 4
    y = 2 * yh + yl
    oc = 1 - c
    s = 1 - 2 * c
    xf, xk, xo = (x + s + 4) % 4, (x - s + 4) % 4, (x + 2) % 4
    zf, zk = (z + s + 8) % 8, (z - s + 8) % 8

    def dev(x_=x, y_=y, z_=z, c_=c):
        return (2 * (y_ % 2) + c_, 4 * x_ + y_ // 2, z_)

    def remote(src, dst, ssem, rsem, to):
        return pltpu.make_async_remote_copy(
            src_ref=src, dst_ref=dst, send_sem=ssem, recv_sem=rsem, device_id=to, device_id_type=MESH
        )

    partner = dev(c_=oc)

    barrier = pltpu.get_barrier_semaphore()

    def greet(to):
        pl.semaphore_signal(barrier, inc=1, device_id=to, device_id_type=MESH)

    greet(partner)
    for k in range(1, 8):
        greet(dev(y_=(y + k) % 8))
        greet(dev(z_=(z + k) % 8))
    for k in range(1, 4):
        greet(dev(x_=(x + k) % 4))
    pl.semaphore_wait(barrier, 18)

    def t1(k):
        d = (yh + k) % 4
        return remote(
            amps.at[d], tb.at[c, x, z, pl.ds(pl.multiple_of(yh * 32, 32), 32)], t1_s.at[k], t1_r,
            dev(y_=2 * d + yl),
        )

    t1_own = pltpu.make_async_copy(amps.at[yh], tb.at[c, x, z, pl.ds(pl.multiple_of(yh * 32, 32), 32)], t1_r)
    for k in range(1, 4):
        t1(k).start()
    t1_own.start()

    half, slot = y // 4, y % 4
    bd_own = pltpu.make_async_copy(chol, bd.at[yl, c, z], bd_r.at[yl, z])
    bd_own.start()
    to_pair = remote(chol, bd.at[yl, c, z], y_s.at[4], bd_r.at[yl, z], dev(y_=y + 1 - 2 * yl))
    to_pair.start()

    def z_send(u, t, forward):
        yq = (yl + u) % 2
        if forward:
            zz = (z - s * t + 8) % 8
            return remote(bd.at[yq, c, zz], bd.at[yq, c, zz], z_s.at[0, u, t], bd_r.at[yq, zz], dev(z_=zf))
        zz = (z + s * t + 8) % 8
        return remote(bd.at[yq, c, zz], bd.at[yq, c, zz], z_s.at[1, u, t], bd_r.at[yq, zz], dev(z_=zk))

    def bd_wait(u, zz):
        yq = (yl + u) % 2
        pltpu.make_async_copy(bd.at[yq, c, zz], bd.at[yq, c, zz], bd_r.at[yq, zz]).wait()

    def bd_share(u, zz):
        yq = (yl + u) % 2
        return remote(bd.at[yq, c, zz], bd.at[yq, c, zz], bdp_s.at[u, zz], bdp_r.at[yq, zz], partner)

    near = [2 * ((yh + k) % 4) + half for k in range(4)]
    for k in (0, 1, 3, 2):
        @pl.when(near[k] != y)
        def _(k=k):
            remote(chol, xb.at[x, slot], y_s.at[k], xb_r.at[x, slot], dev(y_=near[k])).start()

        @pl.when(near[k] == y)
        def _():
            pltpu.make_async_copy(chol, xb.at[x, slot], xb_r.at[x, slot]).start()

    bd_wait(0, z)
    z_send(0, 0, True).start()
    z_send(0, 0, False).start()
    bd_share(0, z).start()
    bd_wait(1, z)
    z_send(1, 0, True).start()
    z_send(1, 0, False).start()
    bd_share(1, z).start()

    pow4 = (1 + 3 * (y % 2)) * (1 + 15 * ((y // 2) % 2)) * (1 + 255 * (y // 4))
    pow2 = (1 + y % 2) * (1 + 3 * ((y // 2) % 2)) * (1 + 15 * (y // 4))
    firsts = sum(f * 4**i for i, f in enumerate((0, 3, 2, 0, 3, 1, 0, 3)))
    downs = sum(f * 2**i for i, f in enumerate((0, 1, 1, 0, 1, 0, 1, 1)))
    h0 = (firsts // pow4) % 4
    hs = 1 - 2 * ((downs // pow2) % 2)
    hs4 = [(h0 + hs * i + 4) % 4 for i in range(4)]

    def x_wait(a, h):
        pltpu.make_async_copy(xb.at[a, h], xb.at[a, h], xb_r.at[a, h]).wait()

    def x_send(a, i, to, which):
        h = hs4[i]
        return remote(xb.at[a, h], xb.at[a, h], x_s.at[which, i], xb_r.at[a, h], dev(x_=to))

    def x_share(a, h):
        return remote(xb.at[a, h], pb.at[a // 2, h], pb_s.at[a // 2, h], pb_r.at[a // 2, h], partner)

    def x_share_if(a, h):
        @pl.when(a % 2 != c)
        def _():
            x_share(a, h).start()

    def t2(k):
        return remote(tb.at[c, x, z], tb.at[c, x, z], t2_s.at[k], t2_r.at[z], dev(z_=(z + k) % 8))

    def tx(a, to, which):
        return remote(tb.at[c, a], tb.at[c, a], tx_s.at[which], tx_r.at[a], dev(x_=to))

    def tx_wait(a):
        pltpu.make_async_copy(tb.at[c, a], tb.at[c, a], tx_r.at[a]).wait()

    def t_share(a):
        return remote(tb.at[c, a], tb.at[c, a], tp_s.at[a], tp_r.at[a], partner)

    for j in range(8):
        if j < 4:
            x_wait(x, hs4[j])
            x_send(x, j, xf, 0).start()
            x_send(x, j, xk, 1).start()
            x_share_if(x, hs4[j])
        if j == 0:
            pltpu.make_async_copy(tb.at[c, x, z], tb.at[c, x, z], t1_r).wait()
            for k in (1, 7, 2, 6, 3, 5, 4):
                t2(k).start()
        u, t = j % 2, j // 2 + 1
        zz = (z - s * t + 8) % 8
        bd_wait(u, zz)
        if t < 4:
            z_send(u, t, True).start()
        bd_share(u, zz).start()
        if t < 4:
            zz = (z + s * t + 8) % 8
            bd_wait(u, zz)
            if t < 3:
                z_send(u, t, False).start()
            bd_share(u, zz).start()
        if j == 3:
            for k in range(1, 8):
                zk_ = (z + k) % 8
                pltpu.make_async_copy(tb.at[c, x, zk_], tb.at[c, x, zk_], t2_r.at[zk_]).wait()
            tx(x, xf, 0).start()
            tx(x, xk, 1).start()
            t_share(x).start()
        if 2 <= j < 6:
            h = hs4[j - 2]
            x_wait(xk, h)
            x_send(xk, j - 2, xf, 2).start()
            x_share_if(xk, h)
            x_wait(xf, h)
            x_share_if(xf, h)
        if j >= 4:
            h = hs4[j - 4]
            x_wait(xo, h)
            x_share_if(xo, h)
    tx_wait(xk)
    tx(xk, xf, 2).start()
    t_share(xk).start()
    tx_wait(xf)
    t_share(xf).start()

    for a in range(2):
        for h in range(4):
            pltpu.make_async_copy(pb.at[a, h], pb.at[a, h], pb_r.at[a, h]).wait()
    for q in range(2):
        for zz in range(8):
            pltpu.make_async_copy(bd.at[q, oc, zz], bd.at[q, oc, zz], bdp_r.at[q, zz]).wait()

    live = [
        [listed[((c + 2 * a) * NTV + 2 * yl + cc) * NTV * NTV + x * NTV + yh].astype(jnp.float32) for a in range(2)]
        for cc in range(2)
    ]

    def integrals(n, carry):
        total = None
        for q in range(2):
            rows = [xb[c + 2 * a, 2 * cc + q] for cc in range(2) for a in range(2)]
            cols = bd[q, c, pl.ds(2 * n, 2)].reshape(256, 512)
            part = lax.dot_general(jnp.concatenate(rows, 0), cols, NT, preferred_element_type=jnp.float32)
            total = part if total is None else total + part
            rows = [pb[a, 2 * cc + q] for cc in range(2) for a in range(2)]
            cols = bd[q, oc, pl.ds(2 * n, 2)].reshape(256, 512)
            total = total + lax.dot_general(
                jnp.concatenate(rows, 0), cols, NT, preferred_element_type=jnp.float32
            )
        for cc in range(2):
            for a in range(2):
                lo = (2 * cc + a) * 128
                block = total[lo : lo + 128] * live[cc][a]
                v[2 * n, pl.ds(lo, 128), :] = block[:, :128]
                v[2 * n + 1, pl.ds(lo, 128), :] = block[:, 128:]
        return carry

    lax.fori_loop(0, 4, integrals, 0)

    group = lax.broadcasted_iota(jnp.int32, (8, 128), 1) // 32
    odd, high = group % 2 == 1, group >= 2

    def swap(i, carry):
        cc, g = i // 8, i % 8
        for zz in range(8):
            r = [v[zz, pl.ds(cc * 256 + 4 * g + j, 8, stride=32), :] for j in range(4)]
            p = [None] * 4
            for j in (0, 2):
                p[j] = jnp.where(odd, pltpu.roll(r[j + 1], 32, 1), r[j])
                p[j + 1] = jnp.where(odd, r[j + 1], pltpu.roll(r[j], 96, 1))
            for j in (0, 1):
                w[i, pl.ds(4 * zz + j, 8, stride=32), :] = jnp.where(high, pltpu.roll(p[j + 2], 64, 1), p[j])
                w[i, pl.ds(4 * zz + j + 2, 8, stride=32), :] = jnp.where(high, p[j + 2], pltpu.roll(p[j], 64, 1))
        return carry

    lax.fori_loop(0, 16, swap, 0)

    tx_wait(xo)
    t_share(xo).start()
    for a in range(4):
        pltpu.make_async_copy(tb.at[oc, a], tb.at[oc, a], tp_r.at[a]).wait()

    def contract(n, carry):
        total = None
        for i in range(0, 16, 2):
            t = jnp.concatenate([tb[i // 8, n, i % 8], tb[i // 8, n, i % 8 + 1]], 1)
            m = jnp.concatenate([w[i].astype(jnp.bfloat16), w[i + 1].astype(jnp.bfloat16)], 1)
            part = lax.dot_general(t, m, NT, preferred_element_type=jnp.float32)
            total = part if total is None else total + part
        total = total.astype(jnp.bfloat16)
        for i in range(4):
            for a in range(2):
                rs[2 * i + a, n] = total[32 * i : 32 * i + 32, 128 * a : 128 * a + 128]
        return carry

    lax.fori_loop(0, 4, contract, 0)

    def r1(k):
        to = (y + k) % 8
        return remote(rs.at[to], rr.at[y], rr_s.at[k], rr_r.at[y], dev(y_=to))

    for k in (1, 7, 2, 6, 3, 5, 4):
        r1(k).start()
    total = rs[y].astype(jnp.float32)
    for k in (1, 7, 2, 6, 3, 5, 4):
        f = (y + k) % 8
        pltpu.make_async_copy(rr.at[f], rr.at[f], rr_r.at[f]).wait()
        total = total + rr[f].astype(jnp.float32)
    rx[...] = total

    def r2(k):
        to = (x + k) % 4
        return remote(rx.at[to], ob.at[x], ob_s.at[k], ob_r.at[x], dev(x_=to))

    for k in (1, 3, 2):
        r2(k).start()
    out[x] = rx[x]

    for k in range(1, 4):
        t1(k).wait_send()
        t2(k).wait_send()
        t2(k + 4).wait_send()
    t2(4).wait_send()
    to_pair.wait_send()
    for k in range(4):
        @pl.when(near[k] != y)
        def _(k=k):
            remote(chol, xb.at[x, slot], y_s.at[k], xb_r.at[x, slot], dev(y_=near[k])).wait_send()
    for u in range(2):
        for t in range(4):
            z_send(u, t, True).wait_send()
            if t < 3:
                z_send(u, t, False).wait_send()
        for zz in range(8):
            bd_share(u, zz).wait_send()
    for i in range(4):
        x_send(x, i, xf, 0).wait_send()
        x_send(x, i, xk, 1).wait_send()
        x_send(xk, i, xf, 2).wait_send()
        t_share(i).wait_send()
        for a in range(2):
            x_share(oc + 2 * a, i).wait_send()
    tx(x, xf, 0).wait_send()
    tx(x, xk, 1).wait_send()
    tx(xk, xf, 2).wait_send()
    for k in range(1, 8):
        r1(k).wait_send()
    for k in range(1, 4):
        r2(k).wait_send()
    for k in (1, 3, 2):
        f = (x + k) % 4
        pltpu.make_async_copy(ob.at[f], ob.at[f], ob_r.at[f]).wait()
        out[f] = ob[f]


def on_device(chol, amps, listed):
    bf16, f32, dma = jnp.bfloat16, jnp.float32, pltpu.SemaphoreType.DMA
    anyspace = pl.BlockSpec(memory_space=pl.ANY)
    out = pl.pallas_call(
        kernel,
        out_shape=jax.ShapeDtypeStruct((4, 32, 128), f32),
        in_specs=[pl.BlockSpec(memory_space=pltpu.SMEM), anyspace, anyspace],
        out_specs=pl.BlockSpec(memory_space=pltpu.VMEM),
        scratch_shapes=[
            pltpu.VMEM((2, 2, 8, 128, 512), bf16),
            pltpu.VMEM((4, 4, 128, 512), bf16),
            pltpu.VMEM((2, 4, 128, 512), bf16),
            pltpu.VMEM((2, 4, 8, 128, 128), bf16),
            pltpu.VMEM((8, 512, 128), f32),
            pltpu.VMEM((16, 256, 128), f32),
            pltpu.VMEM((8, 4, 32, 128), bf16),
            pltpu.VMEM((8, 4, 32, 128), bf16),
            pltpu.VMEM((4, 32, 128), f32),
            pltpu.VMEM((4, 32, 128), f32),
            dma((2, 8)), dma((2, 8)), dma((4, 4)), dma((2, 4)), dma, dma((8,)), dma((4,)), dma((4,)), dma((8,)), dma((4,)),
            dma, dma((5,)), dma((2, 2, 4)), dma((3, 4)), dma((2, 8)), dma((2, 4)), dma((4,)), dma((8,)), dma((3,)), dma((4,)), dma((8,)), dma((4,)),
        ],
        compiler_params=pltpu.CompilerParams(
            collective_id=0, has_side_effects=True, vmem_limit_bytes=60 * 1024 * 1024
        ),
    )(listed.reshape(-1), chol[0], jnp.swapaxes(amps[0], 1, 2))
    return jnp.swapaxes(out, 1, 2)[None]


def solution(mesh):
    placed = (P("right", "occ", "left"), P("left", None, "occ", "right"), P())
    return jax.shard_map(
        on_device,
        mesh=mesh,
        in_specs=placed,
        out_specs=P("left", None, "occ", "right"),
        check_vma=False,
    )
```

```python
import jax
import jax.numpy as jnp
from jax import lax
from jax.experimental import pallas as pl
from jax.experimental.pallas import tpu as pltpu
from jax.sharding import PartitionSpec as P

NTV = 4
MESH = pl.DeviceIdType.MESH
NT = (((1,), (1,)), ((), ()))


def kernel(
    chol, amps, listed, out,
    bd, xb, pb, tb, v, w, rs, rr, rx, ob, perm, live,
    bd_r, bdp_r, xb_r, pb_r, t1_r, t2_r, tx_r, tp_r, rr_r, ob_r, live_r,
    y_s, yf_s, z_s, x_s, bdp_s, pb_s, t1_s, t2_s, tx_s, tp_s, rr_s, ob_s,
):
    left = lax.axis_index("left")
    right = lax.axis_index("right")
    z = lax.axis_index("occ")
    yl, c = left // 2, left % 2
    x, yh = right // 4, right % 4
    y = 2 * yh + yl
    oc = 1 - c
    s = 1 - 2 * c
    xf, xk, xo = (x + s + 4) % 4, (x - s + 4) % 4, (x + 2) % 4
    zf, zk = (z + s + 8) % 8, (z - s + 8) % 8
    slot = y % 4
    ch = (1 + yl + yh % 2 + yh // 2) % 2
    own = (slot == 1) | (slot == 2)

    def dev(x_=x, y_=y, z_=z, c_=c):
        return (2 * (y_ % 2) + c_, 4 * x_ + y_ // 2, z_)

    def remote(src, dst, ssem, rsem, to):
        return pltpu.make_async_remote_copy(
            src_ref=src, dst_ref=dst, send_sem=ssem, recv_sem=rsem, device_id=to, device_id_type=MESH
        )

    def arrived(ref, sem):
        pltpu.make_async_copy(ref, ref, sem).wait()

    partner = dev(c_=oc)
    pair = dev(y_=y + 1 - 2 * yl)

    barrier = pltpu.get_barrier_semaphore()

    def greet(to):
        pl.semaphore_signal(barrier, inc=1, device_id=to, device_id_type=MESH)

    greet(partner)
    for k in range(1, 8):
        greet(dev(y_=(y + k) % 8))
        greet(dev(z_=(z + k) % 8))
    for k in range(1, 4):
        greet(dev(x_=(x + k) % 4))
    bd_own = pltpu.make_async_copy(chol, bd.at[yl, c, z], bd_r.at[yl, z])
    bd_own.start()
    pltpu.make_async_copy(listed, live, live_r).start()

    @pl.when(own)
    def _():
        pltpu.make_async_copy(chol, xb.at[x, slot], xb_r.at[x, slot]).start()

    t_rows = pl.ds(pl.multiple_of(yh * 32, 32), 32)
    @pl.when(ch == yl)
    def _():
        pltpu.make_async_copy(amps.at[yh], tb.at[c, x, z, t_rows], t1_r).start()

    spread = lax.broadcasted_iota(jnp.int32, (256, 256), 1)
    spread = (spread % 32) * 8 + spread // 32 == lax.broadcasted_iota(jnp.int32, (256, 256), 0)
    perm[...] = jnp.where(spread, 1.0, 0.0).astype(jnp.bfloat16)
    pl.semaphore_wait(barrier, 18)

    def t1(k):
        d = (yh + k) % 4
        to = dev(y_=2 * d + (1 + d % 2 + d // 2 + yl) % 2)
        return remote(amps.at[d], tb.at[c, x, z, t_rows], t1_s.at[k], t1_r, to)

    for k in (2, 1, 3):
        t1(k).start()

    @pl.when(ch != yl)
    def _():
        t1(0).start()

    to_pair = remote(chol, bd.at[yl, c, z], y_s.at[2], bd_r.at[yl, z], pair)

    @pl.when(own)
    def _():
        to_pair.start()

    up = y + 1 + (slot // 2) * (1 - slot % 2)
    down = y + 7 - (1 - slot // 2) * (slot % 2)
    near = [remote(chol, xb.at[x, slot], y_s.at[k], xb_r.at[x, slot], dev(y_=to % 8)) for k, to in enumerate((up, down))]
    near[0].start()
    near[1].start()

    def z_send(u, t, forward):
        yq = (yl + u) % 2
        zz = (z - s * t + 8) % 8 if forward else (z + s * t + 8) % 8
        src = chol if (u, t) == (0, 0) else bd.at[yq, c, zz]
        return remote(
            src, bd.at[yq, c, zz], z_s.at[0 if forward else 1, u, t], bd_r.at[yq, zz], dev(z_=zf if forward else zk)
        )

    def bd_wait(u, zz):
        yq = (yl + u) % 2
        arrived(bd.at[yq, c, zz], bd_r.at[yq, zz])

    def bd_share(u, zz):
        yq = (yl + u) % 2
        return remote(bd.at[yq, c, zz], bd.at[yq, c, zz], bdp_s.at[u, zz], bdp_r.at[yq, zz], partner)

    z_send(0, 0, True).start()
    z_send(0, 0, False).start()

    pow4 = (1 + 3 * (slot % 2)) * (1 + 15 * (slot // 2))
    hs4 = [
        sum(h * 4**i for i, h in enumerate(row)) // pow4 % 4
        for row in ((2, 1, 2, 1), (3, 0, 3, 0), (1, 2, 1, 2), (0, 3, 0, 3))
    ]

    def x_wait(a, h):
        arrived(xb.at[a, h], xb_r.at[a, h])

    def x_send(a, i, to, which):
        h = hs4[i]
        return remote(xb.at[a, h], xb.at[a, h], x_s.at[which, i], xb_r.at[a, h], dev(x_=to))

    def x_share(a, h):
        return remote(xb.at[a, h], pb.at[a // 2, h], pb_s.at[a // 2, h], pb_r.at[a // 2, h], partner)

    def x_share_if(a, h):
        @pl.when(a % 2 != c)
        def _():
            x_share(a, h).start()

    def y_pass(i, act):
        h = hs4[i]
        for to, go in ((y + slot, h < slot), (y + 5 + slot, h > slot)):
            @pl.when(own & go)
            def _(to=to):
                act(remote(xb.at[x, h], xb.at[x, h], yf_s.at[i], xb_r.at[x, h], dev(y_=to % 8)))

    def rows_in(i):
        h = hs4[i]
        x_wait(x, h)
        y_pass(i, lambda copy: copy.start())
        x_send(x, i, xf, 0).start()
        x_send(x, i, xk, 1).start()
        x_share_if(x, h)

    def t2(k):
        return remote(tb.at[c, x, z], tb.at[c, x, z], t2_s.at[k], t2_r.at[z], dev(z_=(z + k) % 8))

    def tx(a, to, which):
        return remote(tb.at[c, a], tb.at[c, a], tx_s.at[which], tx_r.at[a], dev(x_=to))

    def tx_wait(a):
        arrived(tb.at[c, a], tx_r.at[a])

    def t_share(a):
        return remote(tb.at[c, a], tb.at[c, a], tp_s.at[a], tp_r.at[a], partner)

    @pl.when(own)
    def _():
        rows_in(0)
        rows_in(1)
        pltpu.make_async_copy(xb.at[x, hs4[1]], bd.at[1 - yl, c, z], bd_r.at[1 - yl, z]).start()

    bd_wait(1, z)
    z_send(1, 0, True).start()
    z_send(1, 0, False).start()

    @pl.when(~own)
    def _():
        rows_in(0)

    bd_wait(0, z)
    bd_share(0, z).start()
    bd_share(1, z).start()

    arrived(tb.at[c, x, z], t1_r)
    for k in (1, 7, 2, 6, 3, 5, 4):
        t2(k).start()

    @pl.when(~own)
    def _():
        rows_in(1)

    def hop(i):
        h = hs4[i]
        x_wait(xk, h)
        x_send(xk, i, xf, 2).start()
        x_share_if(xk, h)
        x_wait(xf, h)
        x_share_if(xf, h)

    def hop2(i):
        h = hs4[i]
        x_wait(xo, h)
        x_share_if(xo, h)

    def zstep(j):
        u, t = j % 2, j // 2 + 1
        zz = (z - s * t + 8) % 8
        bd_wait(u, zz)
        if t < 4:
            z_send(u, t, True).start()
        bd_share(u, zz).start()
        if t < 4:
            zz = (z + s * t + 8) % 8
            bd_wait(u, zz)
            if t < 3:
                z_send(u, t, False).start()
            bd_share(u, zz).start()

    for j in range(6):
        zstep(j)
        if j < 2:
            rows_in(j + 2)
        if j < 4:
            hop(j)
        if j == 3:
            for k in range(1, 8):
                zk_ = (z + k) % 8
                arrived(tb.at[c, x, zk_], t2_r.at[zk_])
            tx(x, xf, 0).start()
            tx(x, xk, 1).start()
            t_share(x).start()
        if 2 <= j < 6:
            hop2(j - 2)

    arrived(live, live_r)
    scale = [
        [live[c + 2 * a, 2 * ch + cc, x, yh].astype(jnp.float32) for a in range(2)]
        for cc in range(2)
    ]
    group = lax.broadcasted_iota(jnp.int32, (8, 128), 1) // 32
    odd, high = group % 2 == 1, group >= 2

    def integrals(za, zb):
        for q in range(2):
            for zz in (za, zb):
                arrived(bd.at[q, oc, zz], bdp_r.at[q, zz])
        total = None
        for q in range(2):
            rows = [xb[c + 2 * a, 2 * cc + q] for cc in range(2) for a in range(2)]
            cols = jnp.concatenate([bd[q, c, za], bd[q, c, zb]], 0)
            part = lax.dot_general(jnp.concatenate(rows, 0), cols, NT, preferred_element_type=jnp.float32)
            total = part if total is None else total + part
            rows = [pb[a, 2 * cc + q] for cc in range(2) for a in range(2)]
            cols = jnp.concatenate([bd[q, oc, za], bd[q, oc, zb]], 0)
            total = total + lax.dot_general(
                jnp.concatenate(rows, 0), cols, NT, preferred_element_type=jnp.float32
            )
        for cc in range(2):
            lo = 256 * cc
            block = jnp.concatenate([total[lo + 128 * a : lo + 128 * a + 128] * scale[cc][a] for a in range(2)], 0)
            block = jnp.dot(perm[...], block.astype(jnp.bfloat16), preferred_element_type=jnp.float32)
            v[0, lo : lo + 256, :] = block[:, :128]
            v[1, lo : lo + 256, :] = block[:, 128:]

        def swap(i, carry):
            for k, zz in enumerate((za, zb)):
                r = [v[k, pl.ds(pl.multiple_of(i * 32 + 8 * j, 8), 8), :] for j in range(4)]
                p = [None] * 4
                for j in (0, 2):
                    p[j] = jnp.where(odd, pltpu.roll(r[j + 1], 32, 1), r[j])
                    p[j + 1] = jnp.where(odd, r[j + 1], pltpu.roll(r[j], 96, 1))
                b = [jnp.where(high, pltpu.roll(p[j + 2], 64, 1), p[j]) for j in (0, 1)]
                b += [jnp.where(high, p[j + 2], pltpu.roll(p[j], 64, 1)) for j in (0, 1)]
                w[i, pl.ds(pl.multiple_of(32 * zz, 32), 32), :] = jnp.concatenate(b, 0).astype(jnp.bfloat16)
            return carry

        lax.fori_loop(0, 16, swap, 0, unroll=8)

    for a in range(2):
        for h in range(4):
            arrived(pb.at[a, h], pb_r.at[a, h])

    def zi(k):
        return (z + s * k + 8) % 8

    zstep(6)
    integrals(z, zi(-1))
    tx_wait(xk)
    tx(xk, xf, 2).start()
    tx_wait(xf)
    t_share(xk).start()
    t_share(xf).start()
    integrals(zi(1), zi(-2))
    zstep(7)
    integrals(zi(2), zi(-3))
    integrals(zi(3), zi(-4))

    def contract(*ns):
        total = None
        for i in range(0, 16, 2):
            t = jnp.concatenate(
                [jnp.concatenate([tb[i // 8, n, i % 8], tb[i // 8, n, i % 8 + 1]], 1) for n in ns], 0
            )
            m = jnp.concatenate([w[i], w[i + 1]], 1)
            part = lax.dot_general(t, m, NT, preferred_element_type=jnp.float32)
            total = part if total is None else total + part
        total = jnp.dot(total.astype(jnp.bfloat16), perm[...], preferred_element_type=jnp.float32)
        total = total.astype(jnp.bfloat16)
        for j, n in enumerate(ns):
            for i in range(4):
                for a in range(2):
                    lo = 128 * j + 32 * i
                    rs[n, 2 * i + a] = total[lo : lo + 32, 128 * a : 128 * a + 128]

    far = (4, 3, 5, 2, 6, 1, 7)

    def r1(n, k):
        to = (y + k) % 8
        return remote(rs.at[n, to], rr.at[n, y], rr_s.at[n, k], rr_r.at[n], dev(y_=to))

    order = (x, xk, xf, xo)
    for ns in (order[:3], order[3:]):
        if len(ns) == 1:
            tx_wait(xo)
            t_share(xo).start()
        for n in ns:
            arrived(tb.at[oc, n], tp_r.at[n])
        contract(*ns)
        for n in ns:
            for k in far:
                r1(n, k).start()

    def r2(n):
        return remote(rx.at[n], ob.at[x], ob_s.at[n], ob_r.at[x], dev(x_=n))

    for i, n in enumerate(order):
        arrived(rr.at[n, pl.ds(0, 7)], rr_r.at[n])
        total = rs[n, y].astype(jnp.float32)
        for k in range(1, 8):
            total = total + rr[n, (y + k) % 8].astype(jnp.float32)
        if i == 0:
            out[x] = total
        else:
            rx[n] = total
            r2(n).start()

    near[0].wait_send()
    near[1].wait_send()

    @pl.when(own)
    def _():
        to_pair.wait_send()

    for k in range(1, 4):
        t1(k).wait_send()

    @pl.when(ch != yl)
    def _():
        t1(0).wait_send()

    for k in range(1, 8):
        t2(k).wait_send()
    for u in range(2):
        for t in range(4):
            z_send(u, t, True).wait_send()
            if t < 3:
                z_send(u, t, False).wait_send()
        for zz in range(8):
            bd_share(u, zz).wait_send()
    for i in range(4):
        y_pass(i, lambda copy: copy.wait_send())
        x_send(x, i, xf, 0).wait_send()
        x_send(x, i, xk, 1).wait_send()
        x_send(xk, i, xf, 2).wait_send()
        t_share(i).wait_send()
        for a in range(2):
            x_share(oc + 2 * a, i).wait_send()
        for k in range(1, 8):
            r1(i, k).wait_send()
    tx(x, xf, 0).wait_send()
    tx(x, xk, 1).wait_send()
    tx(xk, xf, 2).wait_send()
    for n in order[1:]:
        r2(n).wait_send()
    for n in order[1:]:
        arrived(ob.at[n], ob_r.at[n])
        out[n] = ob[n]


def on_device(chol, amps, listed):
    bf16, f32, dma = jnp.bfloat16, jnp.float32, pltpu.SemaphoreType.DMA
    anyspace = pl.BlockSpec(memory_space=pl.ANY)
    out = pl.pallas_call(
        kernel,
        out_shape=jax.ShapeDtypeStruct((4, 32, 128), f32),
        in_specs=[anyspace, anyspace, anyspace],
        out_specs=pl.BlockSpec(memory_space=pltpu.VMEM),
        scratch_shapes=[
            pltpu.VMEM((2, 2, 8, 128, 512), bf16),
            pltpu.VMEM((4, 4, 128, 512), bf16),
            pltpu.VMEM((2, 4, 128, 512), bf16),
            pltpu.VMEM((2, 4, 8, 128, 128), bf16),
            pltpu.VMEM((2, 512, 128), f32),
            pltpu.VMEM((16, 256, 128), bf16),
            pltpu.VMEM((4, 8, 32, 128), bf16),
            pltpu.VMEM((4, 8, 32, 128), bf16),
            pltpu.VMEM((4, 32, 128), f32),
            pltpu.VMEM((4, 32, 128), f32),
            pltpu.VMEM((256, 256), bf16),
            pltpu.SMEM((4, 4, 4, 4), jnp.int32),
            dma((2, 8)), dma((2, 8)), dma((4, 4)), dma((2, 4)), dma, dma((8,)), dma((4,)), dma((4,)), dma((4,)), dma((4,)), dma,
            dma((3,)), dma((4,)), dma((2, 2, 4)), dma((3, 4)), dma((2, 8)), dma((2, 4)), dma((4,)), dma((8,)), dma((3,)), dma((4,)),
            dma((4, 8)), dma((4,)),
        ],
        compiler_params=pltpu.CompilerParams(
            collective_id=0, has_side_effects=True, vmem_limit_bytes=60 * 1024 * 1024
        ),
    )(chol[0], jnp.swapaxes(amps[0], 1, 2), listed)
    return jnp.swapaxes(out, 1, 2)[None]


def solution(mesh):
    placed = (P("right", "occ", "left"), P("left", None, "occ", "right"), P())
    return jax.shard_map(
        on_device,
        mesh=mesh,
        in_specs=placed,
        out_specs=P("left", None, "occ", "right"),
        check_vma=False,
    )
```

```python
import jax
import jax.numpy as jnp
from jax import lax
from jax.experimental import pallas as pl
from jax.experimental.pallas import tpu as pltpu
from jax.sharding import PartitionSpec as P

NTV = 4
MESH = pl.DeviceIdType.MESH
NT = (((1,), (1,)), ((), ()))


def kernel(
    chol, amps, listed, out,
    bd, xb, pb, tb, v, w, rs, rr, perm, live,
    bd_r, bdp_r, xb_r, pb_r, t1_r, t2_r, tx_r, tp_r, rr_r, live_r,
    y_s, yf_s, z_s, x_s, bdp_s, pb_s, t1_s, t2_s, tx_s, tp_s, rr_s,
):
    left = lax.axis_index("left")
    right = lax.axis_index("right")
    z = lax.axis_index("occ")
    yl, c = left // 2, left % 2
    x, yh = right // 4, right % 4
    y = 2 * yh + yl
    oc = 1 - c
    s = 1 - 2 * c
    xf, xk, xo = (x + s + 4) % 4, (x - s + 4) % 4, (x + 2) % 4
    zf, zk = (z + s + 8) % 8, (z - s + 8) % 8
    slot = y % 4
    ch = (1 + yl + yh % 2 + yh // 2) % 2
    own = (slot == 1) | (slot == 2)

    def dev(x_=x, y_=y, z_=z, c_=c):
        return (2 * (y_ % 2) + c_, 4 * x_ + y_ // 2, z_)

    def remote(src, dst, ssem, rsem, to):
        return pltpu.make_async_remote_copy(
            src_ref=src, dst_ref=dst, send_sem=ssem, recv_sem=rsem, device_id=to, device_id_type=MESH
        )

    def arrived(ref, sem):
        pltpu.make_async_copy(ref, ref, sem).wait()

    partner = dev(c_=oc)
    pair = dev(y_=y + 1 - 2 * yl)

    barrier = pltpu.get_barrier_semaphore()

    def greet(to):
        pl.semaphore_signal(barrier, inc=1, device_id=to, device_id_type=MESH)

    greet(partner)
    for k in range(1, 8):
        greet(dev(z_=(z + k) % 8))
    for k in range(1, 32):
        greet(dev(x_=(x + k // 8) % 4, y_=(y + k) % 8))
    bd_own = pltpu.make_async_copy(chol, bd.at[yl, c, z], bd_r.at[yl, z])
    bd_own.start()
    pltpu.make_async_copy(listed, live, live_r).start()

    @pl.when(own)
    def _():
        pltpu.make_async_copy(chol, xb.at[x, slot], xb_r.at[x, slot]).start()

    t_rows = pl.ds(pl.multiple_of(yh * 32, 32), 32)
    @pl.when(ch == yl)
    def _():
        pltpu.make_async_copy(amps.at[yh], tb.at[c, x, z, t_rows], t1_r).start()

    spread = lax.broadcasted_iota(jnp.int32, (256, 256), 1)
    spread = (spread % 32) * 8 + spread // 32 == lax.broadcasted_iota(jnp.int32, (256, 256), 0)
    perm[...] = jnp.where(spread, 1.0, 0.0).astype(jnp.bfloat16)
    pl.semaphore_wait(barrier, 39)

    def t1(k):
        d = (yh + k) % 4
        to = dev(y_=2 * d + (1 + d % 2 + d // 2 + yl) % 2)
        return remote(amps.at[d], tb.at[c, x, z, t_rows], t1_s.at[k], t1_r, to)

    for k in (2, 1, 3):
        t1(k).start()

    @pl.when(ch != yl)
    def _():
        t1(0).start()

    to_pair = remote(chol, bd.at[yl, c, z], y_s.at[2], bd_r.at[yl, z], pair)

    @pl.when(own)
    def _():
        to_pair.start()

    def near(d):
        return remote(chol, xb.at[x, slot], y_s.at[d % 2], xb_r.at[x, slot], dev(y_=(y + 8 + 1 - 2 * d) % 8))

    away = 1 - 2 * yl

    def relay():
        to = dev(y_=(y - away + 8) % 8)
        block = (slot + away + 4) % 4
        return remote(bd.at[1 - yl, c, z], xb.at[x, block], y_s.at[2], xb_r.at[x, block], to)

    def to_near(act):
        @pl.when(own)
        def _():
            act(remote(chol, xb.at[x, slot], y_s.at[0], xb_r.at[x, slot], dev(y_=(y - away + 8) % 8)))

        @pl.when(~own)
        def _():
            act(near(0))
            act(near(1))

    to_near(lambda copy: copy.start())

    def z_send(u, t, forward):
        yq = (yl + u) % 2
        zz = (z - s * t + 8) % 8 if forward else (z + s * t + 8) % 8
        src = chol if (u, t) == (0, 0) else bd.at[yq, c, zz]
        return remote(
            src, bd.at[yq, c, zz], z_s.at[0 if forward else 1, u, t], bd_r.at[yq, zz], dev(z_=zf if forward else zk)
        )

    def bd_wait(u, zz):
        yq = (yl + u) % 2
        arrived(bd.at[yq, c, zz], bd_r.at[yq, zz])

    def bd_share(u, zz):
        yq = (yl + u) % 2
        return remote(bd.at[yq, c, zz], bd.at[yq, c, zz], bdp_s.at[u, zz], bdp_r.at[yq, zz], partner)

    z_send(0, 0, True).start()
    z_send(0, 0, False).start()

    pow4 = (1 + 3 * (slot % 2)) * (1 + 15 * (slot // 2))
    hs4 = [
        sum(h * 4**i for i, h in enumerate(row)) // pow4 % 4
        for row in ((3, 1, 2, 0), (2, 0, 3, 1), (1, 2, 1, 2), (0, 3, 0, 3))
    ]

    def x_wait(a, h):
        arrived(xb.at[a, h], xb_r.at[a, h])

    def x_send(a, i, to, which):
        h = hs4[i]
        return remote(xb.at[a, h], xb.at[a, h], x_s.at[which, i], xb_r.at[a, h], dev(x_=to))

    def x_share(a, h):
        return remote(xb.at[a, h], pb.at[a // 2, h], pb_s.at[a // 2, h], pb_r.at[a // 2, h], partner)

    def x_share_if(a, h):
        @pl.when(a % 2 != c)
        def _():
            x_share(a, h).start()

    def y_pass(i, act):
        h = hs4[i]
        for to, go in ((y + slot, h < slot), (y + 5 + slot, h > slot)):
            @pl.when(own & go)
            def _(to=to):
                act(remote(xb.at[x, h], xb.at[x, h], yf_s.at[i], xb_r.at[x, h], dev(y_=to % 8)))

    def rows_in(i):
        h = hs4[i]
        x_wait(x, h)
        y_pass(i, lambda copy: copy.start())
        x_send(x, i, xf, 0).start()
        x_send(x, i, xk, 1).start()
        x_share_if(x, h)

    def t2(k):
        return remote(tb.at[c, x, z], tb.at[c, x, z], t2_s.at[k], t2_r.at[z], dev(z_=(z + k) % 8))

    def tx(a, to, which):
        return remote(tb.at[c, a], tb.at[c, a], tx_s.at[which], tx_r.at[a], dev(x_=to))

    def tx_wait(a):
        arrived(tb.at[c, a], tx_r.at[a])

    def t_share(a):
        return remote(tb.at[c, a], tb.at[c, a], tp_s.at[a], tp_r.at[a], partner)

    def hop(i):
        h = hs4[i]
        x_wait(xk, h)
        x_send(xk, i, xf, 2).start()
        x_share_if(xk, h)
        x_wait(xf, h)
        x_share_if(xf, h)

    def hop2(i):
        h = hs4[i]
        x_wait(xo, h)
        x_share_if(xo, h)

    def zstep(j):
        u, t = j % 2, j // 2 + 1
        zz = (z - s * t + 8) % 8
        bd_wait(u, zz)
        if t < 4:
            z_send(u, t, True).start()
        bd_share(u, zz).start()
        if t < 4:
            zz = (z + s * t + 8) % 8
            bd_wait(u, zz)
            if t < 3:
                z_send(u, t, False).start()
            bd_share(u, zz).start()

    def amps_out():
        for k in range(1, 8):
            zk_ = (z + k) % 8
            arrived(tb.at[c, x, zk_], t2_r.at[zk_])
        tx(x, xf, 0).start()
        tx(x, xk, 1).start()
        t_share(x).start()

    def pair_out():
        bd_wait(1, z)
        z_send(1, 0, True).start()
        z_send(1, 0, False).start()

    def own_share():
        bd_wait(0, z)
        bd_share(0, z).start()
        bd_share(1, z).start()

    def amps_along():
        arrived(tb.at[c, x, z], t1_r)
        for k in (1, 7, 2, 6, 3, 5, 4):
            t2(k).start()

    @pl.when(own)
    def _():
        rows_in(0)
        rows_in(1)
        pltpu.make_async_copy(xb.at[x, hs4[1]], bd.at[1 - yl, c, z], bd_r.at[1 - yl, z]).start()
        pair_out()
        amps_along()
        own_share()
        zstep(0)
        rows_in(2)
        hop(0)
        zstep(1)
        rows_in(3)
        hop(1)
        zstep(2)
        hop(2)
        hop2(0)
        zstep(3)
        hop(3)
        amps_out()
        hop2(1)
        zstep(4)
        hop2(2)
        zstep(5)
        hop2(3)

    @pl.when(~own)
    def _():
        pair_out()
        relay().start()
        rows_in(0)
        own_share()
        amps_along()
        zstep(0)
        rows_in(1)
        zstep(1)
        hop(0)
        rows_in(2)
        hop(1)
        zstep(2)
        rows_in(3)
        hop2(0)
        hop(2)
        zstep(3)
        hop2(1)
        hop(3)
        amps_out()
        zstep(4)
        hop2(2)
        zstep(5)
        hop2(3)

    arrived(live, live_r)
    scale = [
        [live[c + 2 * a, 2 * ch + cc, x, yh].astype(jnp.float32) for a in range(2)]
        for cc in range(2)
    ]
    group = lax.broadcasted_iota(jnp.int32, (8, 128), 1) // 32
    odd, high = group % 2 == 1, group >= 2

    def integrals(za, zb):
        for q in range(2):
            for zz in (za, zb):
                arrived(bd.at[q, oc, zz], bdp_r.at[q, zz])
        total = None
        for q in range(2):
            rows = [xb[c + 2 * a, 2 * cc + q] for cc in range(2) for a in range(2)]
            cols = jnp.concatenate([bd[q, c, za], bd[q, c, zb]], 0)
            part = lax.dot_general(jnp.concatenate(rows, 0), cols, NT, preferred_element_type=jnp.float32)
            total = part if total is None else total + part
            rows = [pb[a, 2 * cc + q] for cc in range(2) for a in range(2)]
            cols = jnp.concatenate([bd[q, oc, za], bd[q, oc, zb]], 0)
            total = total + lax.dot_general(
                jnp.concatenate(rows, 0), cols, NT, preferred_element_type=jnp.float32
            )
        for cc in range(2):
            lo = 256 * cc
            block = jnp.concatenate([total[lo + 128 * a : lo + 128 * a + 128] * scale[cc][a] for a in range(2)], 0)
            block = jnp.dot(perm[...], block.astype(jnp.bfloat16), preferred_element_type=jnp.float32)
            v[0, lo : lo + 256, :] = block[:, :128]
            v[1, lo : lo + 256, :] = block[:, 128:]

        def swap(i, carry):
            for k, zz in enumerate((za, zb)):
                r = [v[k, pl.ds(pl.multiple_of(i * 32 + 8 * j, 8), 8), :] for j in range(4)]
                p = [None] * 4
                for j in (0, 2):
                    p[j] = jnp.where(odd, pltpu.roll(r[j + 1], 32, 1), r[j])
                    p[j + 1] = jnp.where(odd, r[j + 1], pltpu.roll(r[j], 96, 1))
                b = [jnp.where(high, pltpu.roll(p[j + 2], 64, 1), p[j]) for j in (0, 1)]
                b += [jnp.where(high, p[j + 2], pltpu.roll(p[j], 64, 1)) for j in (0, 1)]
                w[i, pl.ds(pl.multiple_of(32 * zz, 32), 32), :] = jnp.concatenate(b, 0).astype(jnp.bfloat16)
            return carry

        lax.fori_loop(0, 16, swap, 0, unroll=16)

    for a in range(2):
        for h in range(4):
            arrived(pb.at[a, h], pb_r.at[a, h])

    def zi(k):
        return (z + s * k + 8) % 8

    zstep(6)
    tx_wait(xk)
    tx(xk, xf, 2).start()
    t_share(xk).start()
    tx_wait(xf)
    t_share(xf).start()
    zstep(7)
    def rest(k, carry):
        integrals(zi(k), zi(-k - 1))
        return carry

    lax.fori_loop(0, 4, rest, 0)

    def contract(*ns):
        total = None
        for i in range(0, 16, 2):
            t = jnp.concatenate(
                [jnp.concatenate([tb[i // 8, n, i % 8], tb[i // 8, n, i % 8 + 1]], 1) for n in ns], 0
            )
            m = jnp.concatenate([w[i], w[i + 1]], 1)
            part = lax.dot_general(t, m, NT, preferred_element_type=jnp.float32)
            total = part if total is None else total + part
        total = jnp.dot(total.astype(jnp.bfloat16), perm[...], preferred_element_type=jnp.float32)
        total = total.astype(jnp.bfloat16)
        for j, n in enumerate(ns):
            for i in range(4):
                for a in range(2):
                    lo = 128 * j + 32 * i
                    rs[n, 2 * i + a] = total[lo : lo + 32, 128 * a : 128 * a + 128]

    far = (4, 3, 5, 2, 6, 1, 7)

    def r1(n, k):
        to = (y + k) % 8
        return remote(rs.at[n, to], rr.at[x, y], rr_s.at[n, k], rr_r.at[x], dev(x_=n, y_=to))

    order = (x, xk, xf, xo)
    for ns in (order[:3], order[3:]):
        if len(ns) == 1:
            tx_wait(xo)
            t_share(xo).start()
        for n in ns:
            arrived(tb.at[oc, n], tp_r.at[n])
        contract(*ns)
        for n in ns:
            for k in far if n is x else far + (0,):
                r1(n, k).start()

    def add_up(n):
        total = rr[n, 0].astype(jnp.float32)
        for k in range(1, 8):
            total = total + rr[n, k].astype(jnp.float32)
        out[n] = total

    arrived(rr.at[x, pl.ds(0, 7)], rr_r.at[x])
    rr[x, y] = rs[x, y]
    add_up(x)
    for n in order[1:]:
        arrived(rr.at[n], rr_r.at[n])
        add_up(n)

    to_near(lambda copy: copy.wait_send())

    @pl.when(own)
    def _():
        to_pair.wait_send()

    @pl.when(~own)
    def _():
        relay().wait_send()

    for k in range(1, 4):
        t1(k).wait_send()

    @pl.when(ch != yl)
    def _():
        t1(0).wait_send()

    for k in range(1, 8):
        t2(k).wait_send()
    for u in range(2):
        for t in range(4):
            z_send(u, t, True).wait_send()
            if t < 3:
                z_send(u, t, False).wait_send()
        for zz in range(8):
            bd_share(u, zz).wait_send()
    for i in range(4):
        y_pass(i, lambda copy: copy.wait_send())
        x_send(x, i, xf, 0).wait_send()
        x_send(x, i, xk, 1).wait_send()
        x_send(xk, i, xf, 2).wait_send()
        t_share(i).wait_send()
        for a in range(2):
            x_share(oc + 2 * a, i).wait_send()
    tx(x, xf, 0).wait_send()
    tx(x, xk, 1).wait_send()
    tx(xk, xf, 2).wait_send()
    for n in order:
        for k in far if n is x else far + (0,):
            r1(n, k).wait_send()


def on_device(chol, amps, listed):
    bf16, f32, dma = jnp.bfloat16, jnp.float32, pltpu.SemaphoreType.DMA
    anyspace = pl.BlockSpec(memory_space=pl.ANY)
    out = pl.pallas_call(
        kernel,
        out_shape=jax.ShapeDtypeStruct((4, 32, 128), f32),
        in_specs=[anyspace, anyspace, anyspace],
        out_specs=pl.BlockSpec(memory_space=pltpu.VMEM),
        scratch_shapes=[
            pltpu.VMEM((2, 2, 8, 128, 512), bf16),
            pltpu.VMEM((4, 4, 128, 512), bf16),
            pltpu.VMEM((2, 4, 128, 512), bf16),
            pltpu.VMEM((2, 4, 8, 128, 128), bf16),
            pltpu.VMEM((2, 512, 128), f32),
            pltpu.VMEM((16, 256, 128), bf16),
            pltpu.VMEM((4, 8, 32, 128), bf16),
            pltpu.VMEM((4, 8, 32, 128), bf16),
            pltpu.VMEM((256, 256), bf16),
            pltpu.SMEM((4, 4, 4, 4), jnp.int32),
            dma((2, 8)), dma((2, 8)), dma((4, 4)), dma((2, 4)), dma, dma((8,)), dma((4,)), dma((4,)), dma((4,)), dma,
            dma((3,)), dma((4,)), dma((2, 2, 4)), dma((3, 4)), dma((2, 8)), dma((2, 4)), dma((4,)), dma((8,)), dma((3,)), dma((4,)),
            dma((4, 8)),
        ],
        compiler_params=pltpu.CompilerParams(
            collective_id=0, has_side_effects=True, vmem_limit_bytes=60 * 1024 * 1024
        ),
    )(chol[0], jnp.swapaxes(amps[0], 1, 2), listed)
    return jnp.swapaxes(out, 1, 2)[None]


def solution(mesh):
    placed = (P("right", "occ", "left"), P("left", None, "occ", "right"), P())
    return jax.shard_map(
        on_device,
        mesh=mesh,
        in_specs=placed,
        out_specs=P("left", None, "occ", "right"),
        check_vma=False,
    )
```

```python
import jax
import jax.numpy as jnp
from jax import lax
from jax.experimental import pallas as pl
from jax.experimental.pallas import tpu as pltpu
from jax.sharding import PartitionSpec as P

NTV = 4
MESH = pl.DeviceIdType.MESH
NT = (((1,), (1,)), ((), ()))


def kernel(
    chol, amps, listed, out,
    bd, xb, pb, tb, v, w, rs, rr, perm, live,
    bd_r, bdp_r, xb_r, pb_r, t1_r, t2_r, tx_r, tp_r, rr_r, live_r,
    y_s, yf_s, z_s, x_s, bdp_s, pb_s, t1_s, t2_s, tx_s, tp_s, rr_s,
):
    left = lax.axis_index("left")
    right = lax.axis_index("right")
    z = lax.axis_index("occ")
    yl, c = left // 2, left % 2
    x, yh = right // 4, right % 4
    y = 2 * yh + yl
    oc = 1 - c
    s = 1 - 2 * c
    xf, xk, xo = (x + s + 4) % 4, (x - s + 4) % 4, (x + 2) % 4
    zf, zk = (z + s + 8) % 8, (z - s + 8) % 8
    slot = y % 4
    ch = (1 + yl + yh % 2 + yh // 2) % 2
    own = (slot == 1) | (slot == 2)

    def dev(x_=x, y_=y, z_=z, c_=c):
        return (2 * (y_ % 2) + c_, 4 * x_ + y_ // 2, z_)

    def remote(src, dst, ssem, rsem, to):
        return pltpu.make_async_remote_copy(
            src_ref=src, dst_ref=dst, send_sem=ssem, recv_sem=rsem, device_id=to, device_id_type=MESH
        )

    def arrived(ref, sem):
        pltpu.make_async_copy(ref, ref, sem).wait()

    partner = dev(c_=oc)
    pair = dev(y_=y + 1 - 2 * yl)

    barrier = pltpu.get_barrier_semaphore()

    def greet(to):
        pl.semaphore_signal(barrier, inc=1, device_id=to, device_id_type=MESH)

    greet(partner)
    for k in range(1, 8):
        greet(dev(z_=(z + k) % 8))
    for k in range(1, 32):
        greet(dev(x_=(x + k // 8) % 4, y_=(y + k) % 8))
    bd_own = pltpu.make_async_copy(chol, bd.at[yl, c, z], bd_r.at[yl, z])
    bd_own.start()
    pltpu.make_async_copy(listed, live, live_r).start()

    @pl.when(own)
    def _():
        pltpu.make_async_copy(chol, xb.at[x, slot], xb_r.at[x, slot]).start()

    t_rows = pl.ds(pl.multiple_of(yh * 32, 32), 32)
    @pl.when(ch == yl)
    def _():
        pltpu.make_async_copy(amps.at[yh], tb.at[c, x, z, t_rows], t1_r).start()

    spread = lax.broadcasted_iota(jnp.int32, (256, 256), 1)
    spread = (spread % 32) * 8 + spread // 32 == lax.broadcasted_iota(jnp.int32, (256, 256), 0)
    perm[...] = jnp.where(spread, 1.0, 0.0).astype(jnp.bfloat16)
    pl.semaphore_wait(barrier, 39)

    def t1(k):
        d = (yh + k) % 4
        to = dev(y_=2 * d + (1 + d % 2 + d // 2 + yl) % 2)
        return remote(amps.at[d], tb.at[c, x, z, t_rows], t1_s.at[k], t1_r, to)

    for k in (2, 1, 3):
        t1(k).start()

    @pl.when(ch != yl)
    def _():
        t1(0).start()

    to_pair = remote(chol, bd.at[yl, c, z], y_s.at[2], bd_r.at[yl, z], pair)

    @pl.when(own)
    def _():
        to_pair.start()

    def near(d):
        return remote(chol, xb.at[x, slot], y_s.at[d % 2], xb_r.at[x, slot], dev(y_=(y + 8 + 1 - 2 * d) % 8))

    away = 1 - 2 * yl

    def relay():
        to = dev(y_=(y - away + 8) % 8)
        block = (slot + away + 4) % 4
        return remote(bd.at[1 - yl, c, z], xb.at[x, block], y_s.at[2], xb_r.at[x, block], to)

    def to_near(act):
        @pl.when(own)
        def _():
            act(remote(chol, xb.at[x, slot], y_s.at[0], xb_r.at[x, slot], dev(y_=(y - away + 8) % 8)))

        @pl.when(~own)
        def _():
            act(near(0))
            act(near(1))

    to_near(lambda copy: copy.start())

    def z_send(u, t, forward):
        yq = (yl + u) % 2
        zz = (z - s * t + 8) % 8 if forward else (z + s * t + 8) % 8
        src = chol if (u, t) == (0, 0) else bd.at[yq, c, zz]
        return remote(
            src, bd.at[yq, c, zz], z_s.at[0 if forward else 1, u, t], bd_r.at[yq, zz], dev(z_=zf if forward else zk)
        )

    def bd_wait(u, zz):
        yq = (yl + u) % 2
        arrived(bd.at[yq, c, zz], bd_r.at[yq, zz])

    def bd_share(u, zz):
        yq = (yl + u) % 2
        return remote(bd.at[yq, c, zz], bd.at[yq, c, zz], bdp_s.at[u, zz], bdp_r.at[yq, zz], partner)

    z_send(0, 0, True).start()
    z_send(0, 0, False).start()

    pow4 = (1 + 3 * (slot % 2)) * (1 + 15 * (slot // 2))
    hs4 = [
        sum(h * 4**i for i, h in enumerate(row)) // pow4 % 4
        for row in ((3, 1, 2, 0), (2, 0, 3, 1), (1, 2, 1, 2), (0, 3, 0, 3))
    ]

    def x_wait(a, h):
        arrived(xb.at[a, h], xb_r.at[a, h])

    def x_send(a, i, to, which):
        h = hs4[i]
        return remote(xb.at[a, h], xb.at[a, h], x_s.at[which, i], xb_r.at[a, h], dev(x_=to))

    def x_share(a, h):
        return remote(xb.at[a, h], pb.at[a // 2, h], pb_s.at[a // 2, h], pb_r.at[a // 2, h], partner)

    def x_share_if(a, h):
        @pl.when(a % 2 != c)
        def _():
            x_share(a, h).start()

    def y_pass(i, act):
        h = hs4[i]
        for to, go in ((y + slot, h < slot), (y + 5 + slot, h > slot)):
            @pl.when(own & go)
            def _(to=to):
                act(remote(xb.at[x, h], xb.at[x, h], yf_s.at[i], xb_r.at[x, h], dev(y_=to % 8)))

    def rows_in(i):
        h = hs4[i]
        x_wait(x, h)
        y_pass(i, lambda copy: copy.start())
        x_send(x, i, xf, 0).start()
        x_send(x, i, xk, 1).start()
        x_share_if(x, h)

    def t2(k):
        return remote(tb.at[c, x, z], tb.at[c, x, z], t2_s.at[k], t2_r.at[z], dev(z_=(z + k) % 8))

    def tx(a, to, which):
        return remote(tb.at[c, a], tb.at[c, a], tx_s.at[which], tx_r.at[a], dev(x_=to))

    def tx_wait(a):
        arrived(tb.at[c, a], tx_r.at[a])

    def t_share(a):
        return remote(tb.at[c, a], tb.at[c, a], tp_s.at[a], tp_r.at[a], partner)

    def hop(i):
        h = hs4[i]
        x_wait(xk, h)
        x_send(xk, i, xf, 2).start()
        x_share_if(xk, h)
        x_wait(xf, h)
        x_share_if(xf, h)

    def hop2(i):
        h = hs4[i]
        x_wait(xo, h)
        x_share_if(xo, h)

    def zstep(j):
        u, t = j % 2, j // 2 + 1
        zz = (z - s * t + 8) % 8
        bd_wait(u, zz)
        if t < 4:
            z_send(u, t, True).start()
        bd_share(u, zz).start()
        if t < 4:
            zz = (z + s * t + 8) % 8
            bd_wait(u, zz)
            if t < 3:
                z_send(u, t, False).start()
            bd_share(u, zz).start()

    def amps_out():
        for k in range(1, 8):
            zk_ = (z + k) % 8
            arrived(tb.at[c, x, zk_], t2_r.at[zk_])
        tx(x, xf, 0).start()
        tx(x, xk, 1).start()
        t_share(x).start()

    def pair_out():
        bd_wait(1, z)
        z_send(1, 0, True).start()
        z_send(1, 0, False).start()

    def own_share():
        bd_wait(0, z)
        bd_share(0, z).start()
        bd_share(1, z).start()

    def amps_along():
        arrived(tb.at[c, x, z], t1_r)
        for k in (1, 7, 2, 6, 3, 5, 4):
            t2(k).start()

    @pl.when(own)
    def _():
        rows_in(0)
        rows_in(1)
        pltpu.make_async_copy(xb.at[x, hs4[1]], bd.at[1 - yl, c, z], bd_r.at[1 - yl, z]).start()
        pair_out()
        amps_along()
        own_share()
        zstep(0)
        rows_in(2)
        hop(0)
        zstep(1)
        rows_in(3)
        hop(1)
        zstep(2)
        hop(2)
        hop2(0)
        zstep(3)
        hop(3)
        amps_out()
        hop2(1)
        zstep(4)
        hop2(2)
        zstep(5)
        hop2(3)

    @pl.when(~own)
    def _():
        pair_out()
        relay().start()
        rows_in(0)
        own_share()
        amps_along()
        zstep(0)
        rows_in(1)
        zstep(1)
        hop(0)
        rows_in(2)
        hop(1)
        zstep(2)
        rows_in(3)
        hop2(0)
        hop(2)
        zstep(3)
        hop2(1)
        hop(3)
        amps_out()
        zstep(4)
        hop2(2)
        zstep(5)
        hop2(3)

    arrived(live, live_r)
    scale = [
        [live[c + 2 * a, 2 * ch + cc, x, yh].astype(jnp.float32) for a in range(2)]
        for cc in range(2)
    ]
    group = lax.broadcasted_iota(jnp.int32, (8, 128), 1) // 32
    odd, high = group % 2 == 1, group >= 2

    def integrals(za, zb):
        for q in range(2):
            for zz in (za, zb):
                arrived(bd.at[q, oc, zz], bdp_r.at[q, zz])
        total = None
        for q in range(2):
            rows = [xb[c + 2 * a, 2 * cc + q] for cc in range(2) for a in range(2)]
            cols = jnp.concatenate([bd[q, c, za], bd[q, c, zb]], 0)
            part = lax.dot_general(jnp.concatenate(rows, 0), cols, NT, preferred_element_type=jnp.float32)
            total = part if total is None else total + part
            rows = [pb[a, 2 * cc + q] for cc in range(2) for a in range(2)]
            cols = jnp.concatenate([bd[q, oc, za], bd[q, oc, zb]], 0)
            total = total + lax.dot_general(
                jnp.concatenate(rows, 0), cols, NT, preferred_element_type=jnp.float32
            )
        for cc in range(2):
            lo = 256 * cc
            block = jnp.concatenate([total[lo + 128 * a : lo + 128 * a + 128] * scale[cc][a] for a in range(2)], 0)
            block = jnp.dot(perm[...], block.astype(jnp.bfloat16), preferred_element_type=jnp.float32)
            v[0, lo : lo + 256, :] = block[:, :128]
            v[1, lo : lo + 256, :] = block[:, 128:]

        def swap(i, carry):
            for k, zz in enumerate((za, zb)):
                r = [v[k, pl.ds(pl.multiple_of(i * 32 + 8 * j, 8), 8), :] for j in range(4)]
                p = [None] * 4
                for j in (0, 2):
                    p[j] = jnp.where(odd, pltpu.roll(r[j + 1], 32, 1), r[j])
                    p[j + 1] = jnp.where(odd, r[j + 1], pltpu.roll(r[j], 96, 1))
                b = [jnp.where(high, pltpu.roll(p[j + 2], 64, 1), p[j]) for j in (0, 1)]
                b += [jnp.where(high, p[j + 2], pltpu.roll(p[j], 64, 1)) for j in (0, 1)]
                w[i, pl.ds(pl.multiple_of(32 * zz, 32), 32), :] = jnp.concatenate(b, 0).astype(jnp.bfloat16)
            return carry

        lax.fori_loop(0, 16, swap, 0, unroll=16)

    for a in range(2):
        for h in range(4):
            arrived(pb.at[a, h], pb_r.at[a, h])

    def zi(k):
        return (z + s * k + 8) % 8

    zstep(6)

    def piece(k, carry):
        integrals(zi(k), zi(-k - 1))

        @pl.when(k == 0)
        def _():
            tx_wait(xk)
            tx(xk, xf, 2).start()
            t_share(xk).start()
            tx_wait(xf)
            t_share(xf).start()
            zstep(7)

        return carry

    lax.fori_loop(0, 4, piece, 0)

    def contract(*ns):
        total = None
        for i in range(0, 16, 2):
            t = jnp.concatenate(
                [jnp.concatenate([tb[i // 8, n, i % 8], tb[i // 8, n, i % 8 + 1]], 1) for n in ns], 0
            )
            m = jnp.concatenate([w[i], w[i + 1]], 1)
            part = lax.dot_general(t, m, NT, preferred_element_type=jnp.float32)
            total = part if total is None else total + part
        total = jnp.dot(total.astype(jnp.bfloat16), perm[...], preferred_element_type=jnp.float32)
        total = total.astype(jnp.bfloat16)
        for j, n in enumerate(ns):
            for i in range(4):
                for a in range(2):
                    lo = 128 * j + 32 * i
                    rs[n, 2 * i + a] = total[lo : lo + 32, 128 * a : 128 * a + 128]

    far = (4, 3, 5, 2, 6, 1, 7)

    def r1(n, k):
        to = (y + k) % 8
        return remote(rs.at[n, to], rr.at[x, y], rr_s.at[n, k], rr_r.at[x], dev(x_=n, y_=to))

    order = (x, xk, xf, xo)
    for ns in (order[:3], order[3:]):
        if len(ns) == 1:
            tx_wait(xo)
            t_share(xo).start()
        for n in ns:
            arrived(tb.at[oc, n], tp_r.at[n])
        contract(*ns)
        for n in ns:
            for k in far if n is x else far + (0,):
                r1(n, k).start()

    def add_up(n):
        total = rr[n, 0].astype(jnp.float32)
        for k in range(1, 8):
            total = total + rr[n, k].astype(jnp.float32)
        out[n] = total

    arrived(rr.at[x, pl.ds(0, 7)], rr_r.at[x])
    rr[x, y] = rs[x, y]
    add_up(x)
    for n in order[1:]:
        arrived(rr.at[n], rr_r.at[n])
        add_up(n)

    to_near(lambda copy: copy.wait_send())

    @pl.when(own)
    def _():
        to_pair.wait_send()

    @pl.when(~own)
    def _():
        relay().wait_send()

    for k in range(1, 4):
        t1(k).wait_send()

    @pl.when(ch != yl)
    def _():
        t1(0).wait_send()

    for k in range(1, 8):
        t2(k).wait_send()
    for u in range(2):
        for t in range(4):
            z_send(u, t, True).wait_send()
            if t < 3:
                z_send(u, t, False).wait_send()
        for zz in range(8):
            bd_share(u, zz).wait_send()
    for i in range(4):
        y_pass(i, lambda copy: copy.wait_send())
        x_send(x, i, xf, 0).wait_send()
        x_send(x, i, xk, 1).wait_send()
        x_send(xk, i, xf, 2).wait_send()
        t_share(i).wait_send()
        for a in range(2):
            x_share(oc + 2 * a, i).wait_send()
    tx(x, xf, 0).wait_send()
    tx(x, xk, 1).wait_send()
    tx(xk, xf, 2).wait_send()
    for n in order:
        for k in far if n is x else far + (0,):
            r1(n, k).wait_send()


def on_device(chol, amps, listed):
    bf16, f32, dma = jnp.bfloat16, jnp.float32, pltpu.SemaphoreType.DMA
    anyspace = pl.BlockSpec(memory_space=pl.ANY)
    out = pl.pallas_call(
        kernel,
        out_shape=jax.ShapeDtypeStruct((4, 32, 128), f32),
        in_specs=[anyspace, anyspace, anyspace],
        out_specs=pl.BlockSpec(memory_space=pltpu.VMEM),
        scratch_shapes=[
            pltpu.VMEM((2, 2, 8, 128, 512), bf16),
            pltpu.VMEM((4, 4, 128, 512), bf16),
            pltpu.VMEM((2, 4, 128, 512), bf16),
            pltpu.VMEM((2, 4, 8, 128, 128), bf16),
            pltpu.VMEM((2, 512, 128), f32),
            pltpu.VMEM((16, 256, 128), bf16),
            pltpu.VMEM((4, 8, 32, 128), bf16),
            pltpu.VMEM((4, 8, 32, 128), bf16),
            pltpu.VMEM((256, 256), bf16),
            pltpu.SMEM((4, 4, 4, 4), jnp.int32),
            dma((2, 8)), dma((2, 8)), dma((4, 4)), dma((2, 4)), dma, dma((8,)), dma((4,)), dma((4,)), dma((4,)), dma,
            dma((3,)), dma((4,)), dma((2, 2, 4)), dma((3, 4)), dma((2, 8)), dma((2, 4)), dma((4,)), dma((8,)), dma((3,)), dma((4,)),
            dma((4, 8)),
        ],
        compiler_params=pltpu.CompilerParams(
            collective_id=0, has_side_effects=True, vmem_limit_bytes=60 * 1024 * 1024
        ),
    )(chol[0], jnp.swapaxes(amps[0], 1, 2), listed)
    return jnp.swapaxes(out, 1, 2)[None]


def solution(mesh):
    placed = (P("right", "occ", "left"), P("left", None, "occ", "right"), P())
    return jax.shard_map(
        on_device,
        mesh=mesh,
        in_specs=placed,
        out_specs=P("left", None, "occ", "right"),
        check_vma=False,
    )
```
